768 devices in a mesh: dp: 32 (over y, x), row: 6 (over z_lo, core), col: 4 (over z_hi).
Axes of the slice: x: 4, y: 8, z: 12 (z_hi: 4, z_lo: 3; z = z_hi * 3 + z_lo), core: 2. Of those that a mesh axis runs over, the one named last changes fastest.
Arguments:
- attn_heads: bfloat16 [98304, 2304], P(('dp', 'col'), 'row'), may hold values from -6 to 6
- out_weight: bfloat16 [2304, 4096], P('row', 'col'), may hold values from -0.125 to 0.125
- cotangent: bfloat16 [98304, 4096], P(('dp', 'row'), 'col'), may hold values from -6 to 6
Outputs:
- head_grad: bfloat16 [98304, 2304], P(('dp', 'col'), 'row')
- weight_grad: float32 [2304, 4096], P('row', 'col')
The draws below stay inside these ranges and needn't reach their ends.
All inputs are finite; a program needn't handle non-finite values.
Results may differ from the reference program's by a relative error of at most 0.015.
Values may be sent and summed in bfloat16 or wider, within the bound.
No kernel may reach another device: no remote copies, remote signals or barrier semaphores. Data moves between devices by JAX's collectives and lax.ppermute only.
A program may use at most 32 MiB of HBM per device.

```python
import jax
import jax.numpy as jnp
from jax import lax

D = 4096
HQ = 2304
TOKENS = 98304
N_COL = 4


def levels(own_key, dims, split, least, high):
    factor_of = 1.0
    for position, parts in split:
        heights = jax.random.uniform(jax.random.fold_in(jax.random.fold_in(own_key, 6), position), (parts,), jnp.float32, least / len(split), high / len(split))
        factor_of = factor_of * jnp.repeat(jnp.exp(heights), dims[position] // parts).reshape((-1,) + (1,) * (len(dims) - 1 - position))
    return factor_of


def noise(key, extent, spread, bound, split=(), kind=jnp.bfloat16):
    drawn = jax.random.normal(key, extent, jnp.float32) * spread
    if len(split) > 0:
        drawn = levels(key, extent, split, -0.22, 0.18) * drawn
    return jnp.clip(drawn, min=-bound, max=bound).astype(kind)


def setup_inputs(seed: int = 0) -> dict:
    splits = jax.random.split(jax.random.key(seed), 4)
    return {
        "attn_heads": noise(splits[0], (TOKENS, HQ), 1.0, 6.0, ((0, 128), (1, 6))),
        "out_weight": noise(splits[1], (HQ, D), HQ ** -0.5, 0.125, ((0, 6), (1, 4))),
        "cotangent": noise(splits[2], (TOKENS, D), 1.0, 6.0, ((0, 192), (1, 4))),
    }


def reference(attn_heads, out_weight, cotangent):
    width = D // N_COL
    head_sum = jnp.zeros((TOKENS, HQ), jnp.float32)
    for block in range(N_COL):
        cot_block = cotangent[:, block * width:(block + 1) * width]
        weight_block = out_weight[:, block * width:(block + 1) * width]
        partial_block = lax.dot_general(cot_block, weight_block, (((1,), (1,)), ((), ())), preferred_element_type=jnp.float32)
        head_sum = head_sum + partial_block.astype(jnp.bfloat16).astype(jnp.float32)
    head_grad = head_sum.astype(jnp.bfloat16)
    grad_scale = float(TOKENS) ** -0.5
    weight_grad = lax.dot_general(attn_heads, cotangent, (((0,), (0,)), ((), ())), preferred_element_type=jnp.float32) * grad_scale
    return head_grad, weight_grad
```

```python
import jax
import jax.numpy as jnp
from jax import lax
from jax.sharding import Mesh, PartitionSpec as P

Y, X, ZL, CORE, ZH = 8, 4, 3, 2, 4
ROW = ZL * CORE
CHUNKS = 2


def ring(n, step):
    return [(i, (i + step) % n) for i in range(n)]


def spread_pairs(k):
    pairs = []
    for row in range(ROW):
        for col in range(ZH):
            d = ZH * row + (col + k) % ZH
            pairs.append((row * ZH + col, (d % ROW) * ZH + d // ROW))
    return pairs


def dot(a, b, dims):
    return lax.dot_general(a, b, (dims, ((), ())), preferred_element_type=jnp.float32)


def per_device(heads, weight, cot):
    bf16, f32 = jnp.bfloat16, jnp.float32
    xi, yi = lax.axis_index("x"), lax.axis_index("y")
    zl, core, zh = lax.axis_index("zl"), lax.axis_index("core"), lax.axis_index("zh")
    tok, feat = cot.shape
    hid = weight.shape[0]
    blk = tok // ZH
    fc = feat // CHUNKS
    own_tok = heads.shape[0]
    grad_scale = float(own_tok * ZH * Y * X) ** (-0.5)

    wr, wc = hid // Y, feat // X
    w_part = lax.dynamic_slice(weight, (yi * wr, xi * wc), (wr, wc))
    w_part = lax.all_gather(w_part, "zh", axis=0)
    w_all = lax.all_gather(w_part, ("y", "x"), axis=0)
    w_all = w_all.reshape(Y, X, ZH, wr, wc).transpose(0, 3, 2, 1, 4).reshape(hid, ZH, feat)

    cot2 = jnp.concatenate([cot, cot], axis=0)
    cot_sends = lax.dynamic_slice(cot2, (zh * blk, 0), (tok, feat))
    q = (zh * ROW + zl * CORE + core) % ZH
    shift = (ZH - 1 - q) % ZH

    def order(m, c):
        return (m % ZL) * CORE + c

    def head_rows(row):
        return lax.dynamic_slice(heads, (row * blk, 0), (blk, heads.shape[1]))

    rows_own = [order(zl, core), order(zl + 2, core), order(zl + 1, core)]
    rows_oth = [order(zl, 1 - core), order(zl + 2, 1 - core), order(zl + 1, 1 - core)]
    heads_own = jnp.concatenate([head_rows(r) for r in rows_own], axis=0)
    heads_oth = jnp.concatenate([head_rows(r) for r in rows_oth], axis=0)

    owns, oths, xparts = [], [], []
    firsts = []
    for h in range(CHUNKS):
        got = [
            lax.ppermute(cot_sends[k * blk:(k + 1) * blk, h * fc:(h + 1) * fc], ("zl", "core", "zh"), spread_pairs(k))
            for k in range(ZH)
        ]
        firsts.append(got)
    for h in range(CHUNKS):
        got = firsts[h]
        rev = jnp.stack([got[(ZH - 1 - i) % ZH] for i in range(2 * ZH - 1)])
        mine = lax.dynamic_slice(rev, (shift, 0, 0), (ZH, blk, fc))
        mine = mine.transpose(1, 0, 2).reshape(blk, ZH * fc)
        below = lax.ppermute(mine, "zl", ring(ZL, 1))
        above = lax.ppermute(mine, "zl", ring(ZL, 2))
        own = jnp.concatenate([mine, below, above], axis=0)
        oth = lax.ppermute(own, "core", ring(CORE, 1))
        owns.append(own)
        oths.append(oth)
        part = dot(heads_own, own, ((0,), (0,))) + dot(heads_oth, oth, ((0,), (0,)))
        part = part.astype(bf16).reshape(hid, ZH, X, fc // X).transpose(2, 0, 1, 3)
        part = lax.all_to_all(part, "x", 0, 0)
        xparts.append(jnp.sum(part.astype(f32), axis=0).astype(bf16))

    r = jnp.stack(xparts).reshape(CHUNKS, Y, wr, ZH, fc // X).transpose(1, 3, 0, 2, 4)
    r = lax.all_to_all(r.reshape(Y * ZH, CHUNKS, wr, fc // X), ("y", "zh"), 0, 0)
    r = jnp.sum(r.astype(f32), axis=0).astype(bf16)
    r = lax.all_to_all(jnp.broadcast_to(r[None], (Y,) + r.shape), "y", 0, 0)
    r = r.transpose(1, 0, 2, 3).reshape(CHUNKS, hid, fc // X)
    r = lax.all_to_all(jnp.broadcast_to(r[None], (X,) + r.shape), "x", 0, 0)
    weight_grad = r.transpose(2, 1, 0, 3).reshape(hid, feat).astype(f32) * grad_scale

    w_chunks = [w_all[:, :, h * fc:(h + 1) * fc].reshape(hid, ZH * fc) for h in range(CHUNKS)]
    g_own = sum(dot(o, w, ((1,), (1,))) for o, w in zip(owns, w_chunks)).astype(bf16)
    g_oth = sum(dot(o, w, ((1,), (1,))) for o, w in zip(oths, w_chunks)).astype(bf16)
    head_grad = jnp.zeros((own_tok, hid), bf16)
    for rows, g in ((rows_own, g_own), (rows_oth, g_oth)):
        for i, row in enumerate(rows):
            head_grad = lax.dynamic_update_slice(head_grad, g[i * blk:(i + 1) * blk], (row * blk, 0))
    return head_grad, weight_grad


def solution(mesh):
    fine = Mesh(mesh.devices.reshape(Y, X, ZL, CORE, ZH), ("y", "x", "zl", "core", "zh"))
    return jax.shard_map(
        per_device,
        mesh=fine,
        in_specs=(P(("y", "x", "zh"), ("zl", "core")), P(("zl", "core"), "zh"), P(("y", "x", "zl", "core"), "zh")),
        out_specs=(P(("y", "x", "zh"), ("zl", "core")), P(("zl", "core"), "zh")),
        check_vma=False,
    )
```

```python
import jax
import jax.numpy as jnp
from jax import lax
from jax.sharding import Mesh, PartitionSpec as P


Y, X, ZL, CORE, ZH = 8, 4, 3, 2, 4
ROW = ZL * CORE
CHUNKS = 2
LANE = 128
XS = 4


def ring(n, step):
    return [(i, (i + step) % n) for i in range(n)]


def spread_pairs(k):
    pairs = []
    for row in range(ROW):
        for col in range(ZH):
            d = ZH * row + (col + k) % ZH
            pairs.append((row * ZH + col, (d % ROW) * ZH + d // ROW))
    return pairs


def dot(a, b, dims):
    return lax.dot_general(a, b, (dims, ((), ())), preferred_element_type=jnp.float32)


def unroll(pieces, at):
    n = len(pieces)
    rev = jnp.stack([pieces[(n - 1 - i) % n] for i in range(2 * n - 1)])
    return lax.dynamic_slice(rev, (n - 1 - at,) + (0,) * (rev.ndim - 1), (n,) + rev.shape[1:])


def per_device(heads, weight, cot):
    bf16, f32 = jnp.bfloat16, jnp.float32
    xi, yi = lax.axis_index("x"), lax.axis_index("y")
    zl, core, zh = lax.axis_index("zl"), lax.axis_index("core"), lax.axis_index("zh")
    tok, feat = cot.shape
    hid = weight.shape[0]
    blk = tok // ZH
    fc = feat // CHUNKS
    own_tok = heads.shape[0]
    grad_scale = float(own_tok * ZH * Y * X) ** (-0.5)

    wr, wc = hid // Y, feat // X
    w_part = lax.dynamic_slice(weight, (yi * wr, xi * wc), (wr, wc))
    w_far = [lax.ppermute(w_part, "zh", ring(ZH, k)) for k in range(1, ZH)]
    w_cols = unroll([w_part] + w_far, zh)
    w_y = lax.all_to_all(jnp.broadcast_to(w_cols[None], (Y, ZH, wr, wc)), "y", 0, 0)
    w_y = w_y.reshape(Y, ZH, wr, wc // LANE, LANE).transpose(0, 2, 3, 1, 4).reshape(hid, wc * ZH)
    w_far = [lax.ppermute(w_y, "x", ring(X, k)) for k in range(1, X)]
    w_x = unroll([w_y] + w_far, xi)

    cot2 = jnp.concatenate([cot, cot], axis=0)
    cot_sends = lax.dynamic_slice(cot2, (zh * blk, 0), (tok, feat))
    q = (zh * ROW + zl * CORE + core) % ZH

    def order(m, c):
        return (m % ZL) * CORE + c

    def head_rows(row):
        return lax.dynamic_slice(heads, (row * blk, 0), (blk, heads.shape[1]))

    rows_own = [order(zl, core), order(zl + 2, core), order(zl + 1, core)]
    rows_oth = [order(zl, 1 - core), order(zl + 2, 1 - core), order(zl + 1, 1 - core)]
    heads_own = jnp.concatenate([head_rows(r) for r in rows_own], axis=0)
    heads_oth = jnp.concatenate([head_rows(r) for r in rows_oth], axis=0)

    sent = []
    for h in range(CHUNKS):
        sent.append([
            lax.ppermute(cot_sends[k * blk:(k + 1) * blk, h * fc:(h + 1) * fc], ("zl", "core", "zh"), spread_pairs(k))
            for k in range(ZH)
        ])
    near = []
    for h in range(CHUNKS):
        mine = unroll(sent[h], q)
        mine = mine.reshape(ZH, blk, XS, LANE).transpose(1, 2, 0, 3).reshape(blk, ZH * fc)
        near.append([mine] + [lax.ppermute(mine, "zl", ring(ZL, k)) for k in (1, 2)])
    xparts, owns, oths = [], [], []
    for h in range(CHUNKS):
        own = jnp.concatenate(near[h], axis=0)
        oth = lax.ppermute(own, "core", ring(CORE, 1))
        owns.append(own)
        oths.append(oth)
        n = ZH * LANE
        part = jnp.stack([
            (dot(heads_own, own[:, s * n:(s + 1) * n], ((0,), (0,)))
             + dot(heads_oth, oth[:, s * n:(s + 1) * n], ((0,), (0,)))).astype(bf16)
            for s in range(XS)
        ])
        part = lax.all_to_all(part, "x", 0, 0)
        xparts.append(jnp.sum(part.astype(f32), axis=0).astype(bf16))

    r = jnp.stack(xparts).reshape(CHUNKS, Y, wr, ZH, LANE).transpose(1, 3, 0, 2, 4)
    r = lax.all_to_all(r.reshape(Y * ZH, CHUNKS, wr, LANE), ("y", "zh"), 0, 0)
    r = jnp.sum(r.astype(f32), axis=0).astype(bf16)
    r = lax.all_to_all(jnp.broadcast_to(r[None], (Y,) + r.shape), "y", 0, 0)
    r = r.transpose(1, 0, 2, 3).reshape(CHUNKS, hid, LANE)
    r = lax.all_to_all(jnp.broadcast_to(r[None], (X,) + r.shape), "x", 0, 0)
    weight_grad = r.transpose(2, 1, 0, 3).reshape(hid, feat).astype(f32) * grad_scale

    def whole(pieces):
        n = wc * ZH
        return sum(
            dot(pieces[g // 2][:, (g % 2) * n:(g % 2 + 1) * n], w_x[g], ((1,), (1,))) for g in range(X)
        ).astype(bf16)

    head_grad = jnp.zeros((own_tok, hid), bf16)
    for rows, g in ((rows_own, whole(owns)), (rows_oth, whole(oths))):
        for i, row in enumerate(rows):
            head_grad = lax.dynamic_update_slice(head_grad, g[i * blk:(i + 1) * blk], (row * blk, 0))
    return head_grad, weight_grad


def solution(mesh):
    fine = Mesh(mesh.devices.reshape(Y, X, ZL, CORE, ZH), ("y", "x", "zl", "core", "zh"))

    return jax.shard_map(
        per_device,
        mesh=fine,
        in_specs=(P(("y", "x", "zh"), ("zl", "core")), P(("zl", "core"), "zh"), P(("y", "x", "zl", "core"), "zh")),
        out_specs=(P(("y", "x", "zh"), ("zl", "core")), P(("zl", "core"), "zh")),
        check_vma=False,
    )
```

```python
import jax
import jax.numpy as jnp
from jax import lax
from jax.experimental import pallas as pl
from jax.experimental.pallas import tpu as pltpu
from jax.sharding import Mesh, PartitionSpec as P


Y, X, ZL, CORE, ZH = 8, 4, 3, 2, 4
ROW = ZL * CORE
CHUNKS = 2
LANE = 128
XS = 4


SMEM = pl.BlockSpec(memory_space=pltpu.SMEM)
VMEM = pl.BlockSpec(memory_space=pltpu.VMEM)


def ring(n, step):
    return [(i, (i + step) % n) for i in range(n)]


def spread_pairs(k):
    pairs = []
    for row in range(ROW):
        for col in range(ZH):
            d = ZH * row + (col + k) % ZH
            pairs.append((row * ZH + col, (d % ROW) * ZH + d // ROW))
    return pairs


def gather_tokens(got, at):
    blk, feat = got[0].shape
    n = feat // CHUNKS

    def kernel(at_ref, *refs):
        outs = refs[ZH:]
        for col in range(ZH):
            k = (at_ref[0] + (ZH - col)) % ZH
            for i in range(ZH):

                @pl.when(k == i)
                def _():
                    for h in range(CHUNKS):
                        for s in range(XS):
                            to, fro = (s * ZH + col) * LANE, h * n + s * LANE
                            outs[h][:, to:to + LANE] = refs[i][:, fro:fro + LANE]

    return pl.pallas_call(
        kernel,
        out_shape=[jax.ShapeDtypeStruct((blk, ZH * n), got[0].dtype)] * CHUNKS,
        in_specs=[SMEM] + [VMEM] * ZH,
        out_specs=[VMEM] * CHUNKS,
        name="gather_tokens",
    )(at.reshape(1), *got)


def order_heads(heads, rows):
    hid = heads.shape[1]
    n = len(rows[0])
    blk = heads.shape[0] // ROW

    def kernel(rows_ref, src, *outs):
        for o, out in enumerate(outs):
            for i in range(n):
                at = pl.multiple_of(rows_ref[o * n + i] * blk, blk)
                out[:, i * blk:(i + 1) * blk] = src[pl.ds(at, blk), :].T

    return pl.pallas_call(
        kernel,
        out_shape=[jax.ShapeDtypeStruct((hid, n * blk), heads.dtype)] * len(rows),
        in_specs=[SMEM, VMEM],
        out_specs=[VMEM] * len(rows),
        name="order_heads",
    )(jnp.stack([r for group in rows for r in group]), heads)


def spread_cols(pieces, at):
    shape = pieces[0].shape

    def kernel(at_ref, *refs):
        out = refs[-1]
        for col in range(ZH):
            k = (at_ref[0] + (ZH - col)) % ZH
            for i in range(ZH):

                @pl.when(k == i)
                def _():
                    v = refs[i][...]
                    for y in range(Y):
                        out[y, col] = v

    return pl.pallas_call(
        kernel,
        out_shape=jax.ShapeDtypeStruct((Y, ZH) + shape, pieces[0].dtype),
        in_specs=[SMEM] + [VMEM] * ZH,
        out_specs=VMEM,
        name="spread_cols",
    )(at.reshape(1), *pieces)


def weight_rows(pieces):
    _, _, rows, wc = pieces.shape

    def kernel(src, out):
        for y in range(Y):
            for col in range(ZH):
                for s in range(wc // LANE):
                    to = (s * ZH + col) * LANE
                    out[y * rows:(y + 1) * rows, to:to + LANE] = src[y, col, :, s * LANE:(s + 1) * LANE]

    return pl.pallas_call(
        kernel,
        out_shape=jax.ShapeDtypeStruct((Y * rows, ZH * wc), pieces.dtype),
        in_specs=[VMEM],
        out_specs=VMEM,
        name="weight_rows",
    )(pieces)


def weight_part(heads_t, own, oth):
    hid, half = heads_t[0].shape
    n = ZH * LANE

    def kernel(a, b, c, d, out):
        acc = jnp.dot(a[...], c[...], preferred_element_type=jnp.float32)
        acc += jnp.dot(b[...], d[...], preferred_element_type=jnp.float32)
        out[0] = acc.astype(out.dtype)

    return pl.pallas_call(
        kernel,
        grid=(XS,),
        out_shape=jax.ShapeDtypeStruct((XS, hid, n), own.dtype),
        in_specs=[pl.BlockSpec((hid, half), lambda s: (0, 0))] * 2 + [pl.BlockSpec((half, n), lambda s: (0, s))] * 2,
        out_specs=pl.BlockSpec((1, hid, n), lambda s: (s, 0, 0)),
        name="weight_part",
    )(*heads_t, own, oth)


def heads_grad(owns, oths, weights, rows, at):
    half = owns[0].shape[0]
    hid, n = weights[0].shape
    blk = half // len(rows[0])
    count = len(rows[0])

    def kernel(at_ref, rows_ref, *refs):
        sides = (refs[:CHUNKS], refs[CHUNKS:2 * CHUNKS])
        w_refs, out, acc = refs[2 * CHUNKS:2 * CHUNKS + X], refs[-2], refs[-1]
        for o, side in enumerate(sides):
            for k in range(X):
                g = (at_ref[0] + (X - k)) % X
                lo = pl.multiple_of((g % 2) * n, n)
                for h in range(CHUNKS):

                    @pl.when(g // 2 == h)
                    def _():
                        prod = lax.dot_general(
                            side[h][:, pl.ds(lo, n)], w_refs[k][...], (((1,), (1,)), ((), ())),
                            preferred_element_type=jnp.float32,
                        )
                        acc[...] = prod if k == 0 else acc[...] + prod
            for i in range(count):
                to = pl.multiple_of(rows_ref[o * count + i] * blk, blk)
                out[pl.ds(to, blk), :] = acc[i * blk:(i + 1) * blk, :].astype(out.dtype)

    return pl.pallas_call(
        kernel,
        out_shape=jax.ShapeDtypeStruct((2 * half, hid), owns[0].dtype),
        in_specs=[SMEM, SMEM] + [VMEM] * (2 * CHUNKS + X),
        out_specs=VMEM,
        scratch_shapes=[pltpu.VMEM((half, hid), jnp.float32)],
        name="heads_grad",
    )(at.reshape(1), jnp.stack([r for group in rows for r in group]), *owns, *oths, *weights)


def sum_split(parts):
    rows = parts[0].shape[1] // Y

    def kernel(*refs):
        out = refs[-1]
        for h in range(CHUNKS):
            for col in range(ZH):
                v = refs[h][:, :, col * LANE:(col + 1) * LANE].astype(jnp.float32)
                out[0, col, h] = jnp.sum(v, axis=0).astype(out.dtype)

    return pl.pallas_call(
        kernel,
        grid=(Y,),
        out_shape=jax.ShapeDtypeStruct((Y, ZH, CHUNKS, rows, LANE), parts[0].dtype),
        in_specs=[pl.BlockSpec((X, rows, ZH * LANE), lambda y: (0, y, 0))] * CHUNKS,
        out_specs=pl.BlockSpec((1, ZH, CHUNKS, rows, LANE), lambda y: (y, 0, 0, 0, 0)),
        name="sum_split",
    )(*parts)


def spread_sum(parts):
    shape = parts.shape[1:]

    def kernel(src, out):
        total = jnp.sum(src[...].astype(jnp.float32), axis=0).astype(out.dtype)
        for y in range(Y):
            out[y] = total

    return pl.pallas_call(
        kernel,
        out_shape=jax.ShapeDtypeStruct((Y,) + shape, parts.dtype),
        in_specs=[VMEM],
        out_specs=VMEM,
        name="spread_sum",
    )(parts)


def spread_rows(parts):
    rows = parts.shape[2]

    def kernel(src, out):
        for x in range(X):
            for y in range(Y):
                for h in range(CHUNKS):
                    out[x, h, y * rows:(y + 1) * rows] = src[y, h]

    return pl.pallas_call(
        kernel,
        out_shape=jax.ShapeDtypeStruct((X, CHUNKS, Y * rows, LANE), parts.dtype),
        in_specs=[VMEM],
        out_specs=VMEM,
        name="spread_rows",
    )(parts)


def finish(parts, scale):
    hid = parts.shape[2]
    rows = hid // 2

    def kernel(src, out):
        for h in range(CHUNKS):
            for x in range(X):
                at = (h * X + x) * LANE
                out[:, at:at + LANE] = src[x, h].astype(jnp.float32) * scale

    return pl.pallas_call(
        kernel,
        grid=(2,),
        out_shape=jax.ShapeDtypeStruct((hid, CHUNKS * X * LANE), jnp.float32),
        in_specs=[pl.BlockSpec((X, CHUNKS, rows, LANE), lambda i: (0, 0, i, 0))],
        out_specs=pl.BlockSpec((rows, CHUNKS * X * LANE), lambda i: (i, 0)),
        name="finish",
    )(parts)


def per_device(heads, weight, cot):
    xi, yi = lax.axis_index("x"), lax.axis_index("y")
    zl, core, zh = lax.axis_index("zl"), lax.axis_index("core"), lax.axis_index("zh")
    tok, feat = cot.shape
    hid = weight.shape[0]
    blk = tok // ZH
    grad_scale = float(heads.shape[0] * ZH * Y * X) ** (-0.5)

    def order(m, c):
        return (m % ZL) * CORE + c

    rows = [[order(zl, c), order(zl + 2, c), order(zl + 1, c)] for c in (core, 1 - core)]

    cot2 = jnp.concatenate([cot, cot], axis=0)
    cot_sends = lax.dynamic_slice(cot2, (zh * blk, 0), (tok, feat))
    got = [
        lax.ppermute(cot_sends[k * blk:(k + 1) * blk], ("zl", "core", "zh"), spread_pairs(k)) for k in range(ZH)
    ]

    wr, wc = hid // Y, feat // X
    w_part = lax.dynamic_slice(weight, (yi * wr, xi * wc), (wr, wc))
    w_far = [lax.ppermute(w_part, "zh", ring(ZH, k)) for k in range(1, ZH)]
    w_y = spread_cols([w_part] + w_far, zh)
    w_y = lax.all_to_all(w_y, "y", 0, 0)
    w_y = weight_rows(w_y)
    w_x = [w_y] + [lax.ppermute(w_y, "x", ring(X, k)) for k in range(1, X)]

    heads_t = order_heads(heads, rows)

    mine = gather_tokens(got, (zh * ROW + zl * CORE + core) % ZH)
    near = []
    for h in range(CHUNKS):
        near.append([mine[h]] + [lax.ppermute(mine[h], "zl", ring(ZL, k)) for k in (1, 2)])
    parts, owns, oths = [], [], []
    for h in range(CHUNKS):
        own = jnp.concatenate(near[h], axis=0)
        oth = lax.ppermute(own, "core", ring(CORE, 1))
        owns.append(own)
        oths.append(oth)
        part = weight_part(heads_t, own, oth)
        parts.append(lax.all_to_all(part, "x", 0, 0))

    r = sum_split(parts)
    r = lax.all_to_all(r.reshape((Y * ZH,) + r.shape[2:]), ("y", "zh"), 0, 0)
    r = spread_sum(r)
    r = lax.all_to_all(r, "y", 0, 0)
    r = spread_rows(r)
    r = lax.all_to_all(r, "x", 0, 0)
    weight_grad = finish(r, grad_scale)

    head_grad = heads_grad(owns, oths, w_x, rows, xi)
    return head_grad, weight_grad


def solution(mesh):
    fine = Mesh(mesh.devices.reshape(Y, X, ZL, CORE, ZH), ("y", "x", "zl", "core", "zh"))

    return jax.shard_map(
        per_device,
        mesh=fine,
        in_specs=(P(("y", "x", "zh"), ("zl", "core")), P(("zl", "core"), "zh"), P(("y", "x", "zl", "core"), "zh")),
        out_specs=(P(("y", "x", "zh"), ("zl", "core")), P(("zl", "core"), "zh")),
        check_vma=False,
    )
```

```python
import jax
import jax.numpy as jnp
from jax import lax
from jax.experimental import pallas as pl
from jax.experimental.pallas import tpu as pltpu
from jax.sharding import Mesh, PartitionSpec as P


Y, X, ZL, CORE, ZH = 8, 4, 3, 2, 4
ROW = ZL * CORE
CHUNKS = 2
LANE = 128
XS = 4


SMEM = pl.BlockSpec(memory_space=pltpu.SMEM)
VMEM = pl.BlockSpec(memory_space=pltpu.VMEM)


def ring(n, step):
    return [(i, (i + step) % n) for i in range(n)]


def spread_pairs(k):
    pairs = []
    for row in range(ROW):
        for col in range(ZH):
            d = ZH * row + (col + k) % ZH
            pairs.append((row * ZH + col, (d % ROW) * ZH + d // ROW))
    return pairs


def gather_tokens(got, at):
    blk, feat = got[0].shape
    n = feat // CHUNKS

    def kernel(at_ref, *refs):
        outs = refs[ZH:]
        for col in range(ZH):
            k = (at_ref[0] + (ZH - col)) % ZH
            for i in range(ZH):

                @pl.when(k == i)
                def _():
                    for h in range(CHUNKS):
                        for s in range(XS):
                            to, fro = (s * ZH + col) * LANE, h * n + s * LANE
                            outs[h][:, to:to + LANE] = refs[i][:, fro:fro + LANE]

    return pl.pallas_call(
        kernel,
        out_shape=[jax.ShapeDtypeStruct((blk, ZH * n), got[0].dtype)] * CHUNKS,
        in_specs=[SMEM] + [VMEM] * ZH,
        out_specs=[VMEM] * CHUNKS,
        name="gather_tokens",
    )(at.reshape(1), *got)


def order_heads(heads, rows):
    hid = heads.shape[1]
    n = len(rows[0])
    blk = heads.shape[0] // ROW

    def kernel(rows_ref, src, *outs):
        for o, out in enumerate(outs):
            for i in range(n):
                at = pl.multiple_of(rows_ref[o * n + i] * blk, blk)
                out[:, i * blk:(i + 1) * blk] = src[pl.ds(at, blk), :].T

    return pl.pallas_call(
        kernel,
        out_shape=[jax.ShapeDtypeStruct((hid, n * blk), heads.dtype)] * len(rows),
        in_specs=[SMEM, VMEM],
        out_specs=[VMEM] * len(rows),
        name="order_heads",
    )(jnp.stack([r for group in rows for r in group]), heads)


def spread_cols(pieces, at):
    shape = pieces[0].shape

    def kernel(at_ref, *refs):
        out = refs[-1]
        for col in range(ZH):
            k = (at_ref[0] + (ZH - col)) % ZH
            for i in range(ZH):

                @pl.when(k == i)
                def _():
                    v = refs[i][...]
                    for y in range(Y):
                        out[y, col] = v

    return pl.pallas_call(
        kernel,
        out_shape=jax.ShapeDtypeStruct((Y, ZH) + shape, pieces[0].dtype),
        in_specs=[SMEM] + [VMEM] * ZH,
        out_specs=VMEM,
        name="spread_cols",
    )(at.reshape(1), *pieces)


def weight_rows(pieces):
    _, _, rows, wc = pieces.shape

    def kernel(src, out):
        for y in range(Y):
            for col in range(ZH):
                for s in range(wc // LANE):
                    to = (s * ZH + col) * LANE
                    out[y * rows:(y + 1) * rows, to:to + LANE] = src[y, col, :, s * LANE:(s + 1) * LANE]

    return pl.pallas_call(
        kernel,
        out_shape=jax.ShapeDtypeStruct((Y * rows, ZH * wc), pieces.dtype),
        in_specs=[VMEM],
        out_specs=VMEM,
        name="weight_rows",
    )(pieces)


def weight_part(heads_t, own, oth, at):
    hid = heads_t[0].shape[0]
    n = ZH * LANE

    def kernel(at_ref, a, b, c, d, *outs):
        for k in range(X):
            lo = pl.multiple_of((at_ref[0] + k) % X * n, n)
            acc = jnp.dot(a[...], c[:, pl.ds(lo, n)], preferred_element_type=jnp.float32)
            acc += jnp.dot(b[...], d[:, pl.ds(lo, n)], preferred_element_type=jnp.float32)
            outs[k][...] = acc.astype(own.dtype)

    return pl.pallas_call(
        kernel,
        out_shape=[jax.ShapeDtypeStruct((hid, n), own.dtype)] * X,
        in_specs=[SMEM] + [VMEM] * 4,
        out_specs=[VMEM] * X,
        name="weight_part",
    )(at.reshape(1), *heads_t, own, oth)


def heads_grad(owns, oths, weights, rows, at):
    half = owns[0].shape[0]
    hid, n = weights[0].shape
    blk = half // len(rows[0])
    count = len(rows[0])

    def kernel(at_ref, rows_ref, *refs):
        sides = (refs[:CHUNKS], refs[CHUNKS:2 * CHUNKS])
        w_refs, out, acc = refs[2 * CHUNKS:2 * CHUNKS + X], refs[-2], refs[-1]
        for o, side in enumerate(sides):
            for k in range(X):
                g = (at_ref[0] + (X - k)) % X
                lo = pl.multiple_of((g % 2) * n, n)
                for h in range(CHUNKS):

                    @pl.when(g // 2 == h)
                    def _():
                        prod = lax.dot_general(
                            side[h][:, pl.ds(lo, n)], w_refs[k][...], (((1,), (1,)), ((), ())),
                            preferred_element_type=jnp.float32,
                        )
                        acc[...] = prod if k == 0 else acc[...] + prod
            for i in range(count):
                to = pl.multiple_of(rows_ref[o * count + i] * blk, blk)
                out[pl.ds(to, blk), :] = acc[i * blk:(i + 1) * blk, :].astype(out.dtype)

    return pl.pallas_call(
        kernel,
        out_shape=jax.ShapeDtypeStruct((2 * half, hid), owns[0].dtype),
        in_specs=[SMEM, SMEM] + [VMEM] * (2 * CHUNKS + X),
        out_specs=VMEM,
        scratch_shapes=[pltpu.VMEM((half, hid), jnp.float32)],
        name="heads_grad",
    )(at.reshape(1), jnp.stack([r for group in rows for r in group]), *owns, *oths, *weights)


def sum_split(parts):
    hid = parts[0].shape[0]
    rows = hid // Y

    def kernel(*refs):
        out = refs[-1]
        for y in range(Y):
            for col in range(ZH):
                total = None
                for ref in refs[:-1]:
                    v = ref[y * rows:(y + 1) * rows, col * LANE:(col + 1) * LANE].astype(jnp.float32)
                    total = v if total is None else total + v
                out[y, col] = total.astype(out.dtype)

    return pl.pallas_call(
        kernel,
        out_shape=jax.ShapeDtypeStruct((Y, ZH, rows, LANE), parts[0].dtype),
        in_specs=[VMEM] * len(parts),
        out_specs=VMEM,
        name="sum_split",
    )(*parts)


def spread_sum(parts):
    shape = (Y, CHUNKS) + parts[0].shape[1:]

    def kernel(*refs):
        out = refs[-1]
        for h in range(CHUNKS):
            total = jnp.sum(refs[h][...].astype(jnp.float32), axis=0).astype(out.dtype)
            for y in range(Y):
                out[y, h] = total

    return pl.pallas_call(
        kernel,
        out_shape=jax.ShapeDtypeStruct(shape, parts[0].dtype),
        in_specs=[VMEM] * CHUNKS,
        out_specs=VMEM,
        name="spread_sum",
    )(*parts)


def spread_rows(parts):
    rows = parts.shape[2]

    def kernel(src, out):
        for x in range(X):
            for y in range(Y):
                for h in range(CHUNKS):
                    out[x, h, y * rows:(y + 1) * rows] = src[y, h]

    return pl.pallas_call(
        kernel,
        out_shape=jax.ShapeDtypeStruct((X, CHUNKS, Y * rows, LANE), parts.dtype),
        in_specs=[VMEM],
        out_specs=VMEM,
        name="spread_rows",
    )(parts)


def finish(parts, scale):
    hid = parts.shape[2]
    rows = hid // 2

    def kernel(src, out):
        for h in range(CHUNKS):
            for x in range(X):
                at = (h * X + x) * LANE
                out[:, at:at + LANE] = src[x, h].astype(jnp.float32) * scale

    return pl.pallas_call(
        kernel,
        grid=(2,),
        out_shape=jax.ShapeDtypeStruct((hid, CHUNKS * X * LANE), jnp.float32),
        in_specs=[pl.BlockSpec((X, CHUNKS, rows, LANE), lambda i: (0, 0, i, 0))],
        out_specs=pl.BlockSpec((rows, CHUNKS * X * LANE), lambda i: (i, 0)),
        name="finish",
    )(parts)


def per_device(heads, weight, cot):
    xi, yi = lax.axis_index("x"), lax.axis_index("y")
    zl, core, zh = lax.axis_index("zl"), lax.axis_index("core"), lax.axis_index("zh")
    tok, feat = cot.shape
    hid = weight.shape[0]
    blk = tok // ZH
    grad_scale = float(heads.shape[0] * ZH * Y * X) ** (-0.5)

    def order(m, c):
        return (m % ZL) * CORE + c

    rows = [[order(zl, c), order(zl + 2, c), order(zl + 1, c)] for c in (core, 1 - core)]

    cot2 = jnp.concatenate([cot, cot], axis=0)
    cot_sends = lax.dynamic_slice(cot2, (zh * blk, 0), (tok, feat))
    got = [
        lax.ppermute(cot_sends[k * blk:(k + 1) * blk], ("zl", "core", "zh"), spread_pairs(k)) for k in range(ZH)
    ]

    wr, wc = hid // Y, feat // X
    w_part = lax.dynamic_slice(weight, (yi * wr, xi * wc), (wr, wc))
    w_far = [lax.ppermute(w_part, "zh", ring(ZH, k)) for k in range(1, ZH)]
    w_y = spread_cols([w_part] + w_far, zh)
    w_y = lax.all_to_all(w_y, "y", 0, 0)
    w_y = weight_rows(w_y)
    w_x = [w_y] + [lax.ppermute(w_y, "x", ring(X, k)) for k in range(1, X)]

    heads_t = order_heads(heads, rows)

    mine = gather_tokens(got, (zh * ROW + zl * CORE + core) % ZH)
    near = []
    for h in range(CHUNKS):
        near.append([mine[h]] + [lax.ppermute(mine[h], "zl", ring(ZL, k)) for k in (1, 2)])
    parts, owns, oths = [], [], []
    for h in range(CHUNKS):
        own = jnp.concatenate(near[h], axis=0)
        oth = lax.ppermute(own, "core", ring(CORE, 1))
        owns.append(own)
        oths.append(oth)
        part = weight_part(heads_t, own, oth, xi)
        parts.append([part[0]] + [lax.ppermute(part[k], "x", ring(X, k)) for k in range(1, X)])
    sums = []
    for h in range(CHUNKS):
        r = sum_split(parts[h])
        sums.append(lax.all_to_all(r.reshape((Y * ZH,) + r.shape[2:]), ("y", "zh"), 0, 0))
    r = spread_sum(sums)
    r = lax.all_to_all(r, "y", 0, 0)
    r = spread_rows(r)
    r = lax.all_to_all(r, "x", 0, 0)
    weight_grad = finish(r, grad_scale)

    head_grad = heads_grad(owns, oths, w_x, rows, xi)
    return head_grad, weight_grad


def solution(mesh):
    fine = Mesh(mesh.devices.reshape(Y, X, ZL, CORE, ZH), ("y", "x", "zl", "core", "zh"))

    return jax.shard_map(
        per_device,
        mesh=fine,
        in_specs=(P(("y", "x", "zh"), ("zl", "core")), P(("zl", "core"), "zh"), P(("y", "x", "zl", "core"), "zh")),
        out_specs=(P(("y", "x", "zh"), ("zl", "core")), P(("zl", "core"), "zh")),
        check_vma=False,
    )
```

```python
import jax
import jax.numpy as jnp
from jax import lax
from jax.experimental import pallas as pl
from jax.experimental.pallas import tpu as pltpu
from jax.sharding import Mesh, PartitionSpec as P


Y, X, ZL, CORE, ZH = 8, 4, 3, 2, 4
ROW = ZL * CORE
CHUNKS = 2
LANE = 128
XS = 4


SMEM = pl.BlockSpec(memory_space=pltpu.SMEM)
VMEM = pl.BlockSpec(memory_space=pltpu.VMEM)


def ring(n, step):
    return [(i, (i + step) % n) for i in range(n)]


def spread_pairs(k):
    pairs = []
    for row in range(ROW):
        for col in range(ZH):
            d = ZH * row + (col + k) % ZH
            pairs.append((row * ZH + col, (d % ROW) * ZH + d // ROW))
    return pairs


def gather_tokens(got, at):
    blk, feat = got[0].shape
    n = feat // CHUNKS

    def kernel(at_ref, *refs):
        outs = refs[ZH:]
        for col in range(ZH):
            k = (at_ref[0] + (ZH - col)) % ZH
            for i in range(ZH):

                @pl.when(k == i)
                def _():
                    for h in range(CHUNKS):
                        for s in range(XS):
                            to, fro = (s * ZH + col) * LANE, h * n + s * LANE
                            outs[h][:, to:to + LANE] = refs[i][:, fro:fro + LANE]

    return pl.pallas_call(
        kernel,
        out_shape=[jax.ShapeDtypeStruct((blk, ZH * n), got[0].dtype)] * CHUNKS,
        in_specs=[SMEM] + [VMEM] * ZH,
        out_specs=[VMEM] * CHUNKS,
        name="gather_tokens",
    )(at.reshape(1), *got)


def order_heads(heads, rows):
    hid = heads.shape[1]
    n = len(rows[0])
    blk = heads.shape[0] // ROW

    def kernel(rows_ref, src, *outs):
        for o, out in enumerate(outs):
            for i in range(n):
                at = pl.multiple_of(rows_ref[o * n + i] * blk, blk)
                out[:, i * blk:(i + 1) * blk] = src[pl.ds(at, blk), :].T

    return pl.pallas_call(
        kernel,
        out_shape=[jax.ShapeDtypeStruct((hid, n * blk), heads.dtype)] * len(rows),
        in_specs=[SMEM, VMEM],
        out_specs=[VMEM] * len(rows),
        name="order_heads",
    )(jnp.stack([r for group in rows for r in group]), heads)


def spread_cols(pieces, at):
    shape = pieces[0].shape

    def kernel(at_ref, *refs):
        out = refs[-1]
        for col in range(ZH):
            k = (at_ref[0] + (ZH - col)) % ZH
            for i in range(ZH):

                @pl.when(k == i)
                def _():
                    v = refs[i][...]
                    for y in range(Y):
                        out[y, col] = v

    return pl.pallas_call(
        kernel,
        out_shape=jax.ShapeDtypeStruct((Y, ZH) + shape, pieces[0].dtype),
        in_specs=[SMEM] + [VMEM] * ZH,
        out_specs=VMEM,
        name="spread_cols",
    )(at.reshape(1), *pieces)


def weight_rows(pieces):
    _, _, rows, wc = pieces.shape

    def kernel(src, out):
        for y in range(Y):
            for col in range(ZH):
                for s in range(wc // LANE):
                    to = (s * ZH + col) * LANE
                    out[y * rows:(y + 1) * rows, to:to + LANE] = src[y, col, :, s * LANE:(s + 1) * LANE]

    return pl.pallas_call(
        kernel,
        out_shape=jax.ShapeDtypeStruct((Y * rows, ZH * wc), pieces.dtype),
        in_specs=[VMEM],
        out_specs=VMEM,
        name="weight_rows",
    )(pieces)


def weight_part(heads_t, own, oth, at):
    hid = heads_t[0].shape[0]
    n = ZH * LANE

    def kernel(at_ref, a, b, c, d, *outs):
        for k in range(X):
            lo = pl.multiple_of((at_ref[0] + k) % X * n, n)
            acc = jnp.dot(a[...], c[:, pl.ds(lo, n)], preferred_element_type=jnp.float32)
            acc += jnp.dot(b[...], d[:, pl.ds(lo, n)], preferred_element_type=jnp.float32)
            outs[k][...] = acc.astype(own.dtype)

    return pl.pallas_call(
        kernel,
        out_shape=[jax.ShapeDtypeStruct((hid, n), own.dtype)] * X,
        in_specs=[SMEM] + [VMEM] * 4,
        out_specs=[VMEM] * X,
        name="weight_part",
    )(at.reshape(1), *heads_t, own, oth)


def heads_grad(owns, oths, weights, rows, at):
    half = owns[0].shape[0]
    hid, n = weights[0].shape
    blk = half // len(rows[0])
    count = len(rows[0])

    def kernel(at_ref, rows_ref, *refs):
        sides = (refs[:CHUNKS], refs[CHUNKS:2 * CHUNKS])
        w_refs, out, acc = refs[2 * CHUNKS:2 * CHUNKS + X], refs[-2], refs[-1]
        for o, side in enumerate(sides):
            for k in range(X):
                g = (at_ref[0] + (X - k)) % X
                lo = pl.multiple_of((g % 2) * n, n)
                for h in range(CHUNKS):

                    @pl.when(g // 2 == h)
                    def _():
                        prod = lax.dot_general(
                            side[h][:, pl.ds(lo, n)], w_refs[k][...], (((1,), (1,)), ((), ())),
                            preferred_element_type=jnp.float32,
                        )
                        acc[...] = prod if k == 0 else acc[...] + prod
            for i in range(count):
                to = pl.multiple_of(rows_ref[o * count + i] * blk, blk)
                out[pl.ds(to, blk), :] = acc[i * blk:(i + 1) * blk, :].astype(out.dtype)

    return pl.pallas_call(
        kernel,
        out_shape=jax.ShapeDtypeStruct((2 * half, hid), owns[0].dtype),
        in_specs=[SMEM, SMEM] + [VMEM] * (2 * CHUNKS + X),
        out_specs=VMEM,
        scratch_shapes=[pltpu.VMEM((half, hid), jnp.float32)],
        name="heads_grad",
    )(at.reshape(1), jnp.stack([r for group in rows for r in group]), *owns, *oths, *weights)


def sum_split(parts):
    hid = parts[0].shape[0]
    rows = hid // Y

    def kernel(*refs):
        out = refs[-1]
        for y in range(Y):
            for col in range(ZH):
                total = None
                for ref in refs[:-1]:
                    v = ref[y * rows:(y + 1) * rows, col * LANE:(col + 1) * LANE].astype(jnp.float32)
                    total = v if total is None else total + v
                out[y, col] = total.astype(out.dtype)

    return pl.pallas_call(
        kernel,
        out_shape=jax.ShapeDtypeStruct((Y, ZH, rows, LANE), parts[0].dtype),
        in_specs=[VMEM] * len(parts),
        out_specs=VMEM,
        name="sum_split",
    )(*parts)


def sum_rows(parts):
    _, _, rows, _ = parts[0].shape

    def kernel(*refs):
        out = refs[-1]
        for h in range(CHUNKS):
            for col in range(ZH):
                out[col, h] = jnp.sum(refs[h][:, col].astype(jnp.float32), axis=0).astype(out.dtype)

    return pl.pallas_call(
        kernel,
        out_shape=jax.ShapeDtypeStruct((ZH, CHUNKS, rows, LANE), parts[0].dtype),
        in_specs=[VMEM] * CHUNKS,
        out_specs=VMEM,
        name="sum_rows",
    )(*parts)


def spread_sum(parts):
    shape = (Y,) + parts.shape[1:]

    def kernel(src, out):
        total = jnp.sum(src[...].astype(jnp.float32), axis=0).astype(out.dtype)
        for y in range(Y):
            out[y] = total

    return pl.pallas_call(
        kernel,
        out_shape=jax.ShapeDtypeStruct(shape, parts.dtype),
        in_specs=[VMEM],
        out_specs=VMEM,
        name="spread_sum",
    )(parts)


def spread_rows(parts):
    rows = parts.shape[2]

    def kernel(src, out):
        for x in range(X):
            for y in range(Y):
                for h in range(CHUNKS):
                    out[x, h, y * rows:(y + 1) * rows] = src[y, h]

    return pl.pallas_call(
        kernel,
        out_shape=jax.ShapeDtypeStruct((X, CHUNKS, Y * rows, LANE), parts.dtype),
        in_specs=[VMEM],
        out_specs=VMEM,
        name="spread_rows",
    )(parts)


def finish(parts, scale):
    hid = parts.shape[2]
    rows = hid // 2

    def kernel(src, out):
        for h in range(CHUNKS):
            for x in range(X):
                at = (h * X + x) * LANE
                out[:, at:at + LANE] = src[x, h].astype(jnp.float32) * scale

    return pl.pallas_call(
        kernel,
        grid=(2,),
        out_shape=jax.ShapeDtypeStruct((hid, CHUNKS * X * LANE), jnp.float32),
        in_specs=[pl.BlockSpec((X, CHUNKS, rows, LANE), lambda i: (0, 0, i, 0))],
        out_specs=pl.BlockSpec((rows, CHUNKS * X * LANE), lambda i: (i, 0)),
        name="finish",
    )(parts)


def per_device(heads, weight, cot):
    xi, yi = lax.axis_index("x"), lax.axis_index("y")
    zl, core, zh = lax.axis_index("zl"), lax.axis_index("core"), lax.axis_index("zh")
    tok, feat = cot.shape
    hid = weight.shape[0]
    blk = tok // ZH
    grad_scale = float(heads.shape[0] * ZH * Y * X) ** (-0.5)

    def order(m, c):
        return (m % ZL) * CORE + c

    rows = [[order(zl, c), order(zl + 2, c), order(zl + 1, c)] for c in (core, 1 - core)]

    sends = [lax.dynamic_slice(cot, ((zh + k) % ZH * blk, 0), (blk, feat)) for k in range(ZH)]
    got = [lax.ppermute(sends[k], ("zl", "core", "zh"), spread_pairs(k)) for k in range(ZH)]

    wr, wc = hid // Y, feat // X
    w_part = lax.dynamic_slice(weight, (yi * wr, xi * wc), (wr, wc))
    w_far = [lax.ppermute(w_part, "zh", ring(ZH, k)) for k in range(1, ZH)]
    w_y = spread_cols([w_part] + w_far, zh)
    w_y = lax.all_to_all(w_y, "y", 0, 0)
    w_y = weight_rows(w_y)
    w_x = [w_y] + [lax.ppermute(w_y, "x", ring(X, k)) for k in range(1, X)]

    heads_t = order_heads(heads, rows)

    mine = gather_tokens(got, (zh * ROW + zl * CORE + core) % ZH)
    near = []
    for h in range(CHUNKS):
        near.append([mine[h]] + [lax.ppermute(mine[h], "zl", ring(ZL, k)) for k in (1, 2)])
    parts, owns, oths = [], [], []
    for h in range(CHUNKS):
        own = jnp.concatenate(near[h], axis=0)
        oth = lax.ppermute(own, "core", ring(CORE, 1))
        owns.append(own)
        oths.append(oth)
        part = weight_part(heads_t, own, oth, xi)
        parts.append([part[0]] + [lax.ppermute(part[k], "x", ring(X, k)) for k in range(1, X)])
    sums = []
    for h in range(CHUNKS):
        r = sum_split(parts[h])
        sums.append(lax.all_to_all(r, "y", 0, 0))
    r = sum_rows(sums)
    r = lax.all_to_all(r, "zh", 0, 0)
    r = spread_sum(r)
    r = lax.all_to_all(r, "y", 0, 0)
    r = spread_rows(r)
    r = lax.all_to_all(r, "x", 0, 0)
    weight_grad = finish(r, grad_scale)

    head_grad = heads_grad(owns, oths, w_x, rows, xi)
    return head_grad, weight_grad


def solution(mesh):
    fine = Mesh(mesh.devices.reshape(Y, X, ZL, CORE, ZH), ("y", "x", "zl", "core", "zh"))

    return jax.shard_map(
        per_device,
        mesh=fine,
        in_specs=(P(("y", "x", "zh"), ("zl", "core")), P(("zl", "core"), "zh"), P(("y", "x", "zl", "core"), "zh")),
        out_specs=(P(("y", "x", "zh"), ("zl", "core")), P(("zl", "core"), "zh")),
        check_vma=False,
    )
```

```python
import jax
import jax.numpy as jnp
from jax import lax
from jax.experimental import pallas as pl
from jax.experimental.pallas import tpu as pltpu
from jax.sharding import Mesh, PartitionSpec as P


Y, X, ZL, CORE, ZH = 8, 4, 3, 2, 4
ROW = ZL * CORE
CHUNKS = 2
LANE = 128
XS = 4


SMEM = pl.BlockSpec(memory_space=pltpu.SMEM)
VMEM = pl.BlockSpec(memory_space=pltpu.VMEM)


def ring(n, step):
    return [(i, (i + step) % n) for i in range(n)]


def spread_pairs(k):
    pairs = []
    for row in range(ROW):
        for col in range(ZH):
            d = ZH * row + (col + k) % ZH
            pairs.append((row * ZH + col, (d % ROW) * ZH + d // ROW))
    return pairs


def gather_tokens(got, at):
    blk, feat = got[0].shape
    n = feat // CHUNKS

    def kernel(at_ref, *refs):
        outs = refs[ZH:]
        for col in range(ZH):
            k = (at_ref[0] + (ZH - col)) % ZH
            for i in range(ZH):

                @pl.when(k == i)
                def _():
                    for h in range(CHUNKS):
                        for s in range(XS):
                            to, fro = (s * ZH + col) * LANE, h * n + s * LANE
                            outs[h][:, to:to + LANE] = refs[i][:, fro:fro + LANE]

    return pl.pallas_call(
        kernel,
        out_shape=[jax.ShapeDtypeStruct((blk, ZH * n), got[0].dtype)] * CHUNKS,
        in_specs=[SMEM] + [VMEM] * ZH,
        out_specs=[VMEM] * CHUNKS,
        name="gather_tokens",
    )(at.reshape(1), *got)


def order_heads(heads, rows):
    hid = heads.shape[1]
    n = len(rows[0])
    blk = heads.shape[0] // ROW

    def kernel(rows_ref, src, *outs):
        for o, out in enumerate(outs):
            for i in range(n):
                at = pl.multiple_of(rows_ref[o * n + i] * blk, blk)
                out[:, i * blk:(i + 1) * blk] = src[pl.ds(at, blk), :].T

    return pl.pallas_call(
        kernel,
        out_shape=[jax.ShapeDtypeStruct((hid, n * blk), heads.dtype)] * len(rows),
        in_specs=[SMEM, VMEM],
        out_specs=[VMEM] * len(rows),
        name="order_heads",
    )(jnp.stack([r for group in rows for r in group]), heads)


def spread_cols(pieces, at):
    shape = pieces[0].shape

    def kernel(at_ref, *refs):
        out = refs[-1]
        for col in range(ZH):
            k = (at_ref[0] + (ZH - col)) % ZH
            for i in range(ZH):

                @pl.when(k == i)
                def _():
                    v = refs[i][...]
                    for y in range(Y):
                        out[y, col] = v

    return pl.pallas_call(
        kernel,
        out_shape=jax.ShapeDtypeStruct((Y, ZH) + shape, pieces[0].dtype),
        in_specs=[SMEM] + [VMEM] * ZH,
        out_specs=VMEM,
        name="spread_cols",
    )(at.reshape(1), *pieces)


def weight_rows(pieces):
    _, _, rows, wc = pieces.shape

    def kernel(src, out):
        for y in range(Y):
            for col in range(ZH):
                for s in range(wc // LANE):
                    to = (s * ZH + col) * LANE
                    out[y * rows:(y + 1) * rows, to:to + LANE] = src[y, col, :, s * LANE:(s + 1) * LANE]

    return pl.pallas_call(
        kernel,
        out_shape=jax.ShapeDtypeStruct((Y * rows, ZH * wc), pieces.dtype),
        in_specs=[VMEM],
        out_specs=VMEM,
        name="weight_rows",
    )(pieces)


def weight_part(heads_t, own, oth, at):
    hid = heads_t[0].shape[0]
    n = ZH * LANE

    def kernel(at_ref, a, b, c, d, *outs):
        for k in range(X):
            lo = pl.multiple_of((at_ref[0] + k) % X * n, n)
            acc = jnp.dot(a[...], c[:, pl.ds(lo, n)], preferred_element_type=jnp.float32)
            acc += jnp.dot(b[...], d[:, pl.ds(lo, n)], preferred_element_type=jnp.float32)
            outs[k][...] = acc.astype(own.dtype)

    return pl.pallas_call(
        kernel,
        out_shape=[jax.ShapeDtypeStruct((hid, n), own.dtype)] * X,
        in_specs=[SMEM] + [VMEM] * 4,
        out_specs=[VMEM] * X,
        name="weight_part",
    )(at.reshape(1), *heads_t, own, oth)


def weight_stack(heads_t, own, oth):
    hid = heads_t[0].shape[0]
    n = ZH * LANE

    def kernel(a, b, c, d, out):
        for x in range(X):
            acc = jnp.dot(a[...], c[:, x * n:(x + 1) * n], preferred_element_type=jnp.float32)
            acc += jnp.dot(b[...], d[:, x * n:(x + 1) * n], preferred_element_type=jnp.float32)
            out[x] = acc.astype(out.dtype)

    return pl.pallas_call(
        kernel,
        out_shape=jax.ShapeDtypeStruct((X, hid, n), own.dtype),
        in_specs=[VMEM] * 4,
        out_specs=VMEM,
        name="weight_stack",
    )(*heads_t, own, oth)


def heads_grad(owns, oths, weights, rows, at):
    half = owns[0].shape[0]
    hid, n = weights[0].shape
    blk = half // len(rows[0])
    count = len(rows[0])

    def kernel(at_ref, rows_ref, *refs):
        sides = (refs[:CHUNKS], refs[CHUNKS:2 * CHUNKS])
        w_refs, out, acc = refs[2 * CHUNKS:2 * CHUNKS + X], refs[-2], refs[-1]
        for o, side in enumerate(sides):
            for k in range(X):
                g = (at_ref[0] + (X - k)) % X
                lo = pl.multiple_of((g % 2) * n, n)
                for h in range(CHUNKS):

                    @pl.when(g // 2 == h)
                    def _():
                        prod = lax.dot_general(
                            side[h][:, pl.ds(lo, n)], w_refs[k][...], (((1,), (1,)), ((), ())),
                            preferred_element_type=jnp.float32,
                        )
                        acc[...] = prod if k == 0 else acc[...] + prod
            for i in range(count):
                to = pl.multiple_of(rows_ref[o * count + i] * blk, blk)
                out[pl.ds(to, blk), :] = acc[i * blk:(i + 1) * blk, :].astype(out.dtype)

    return pl.pallas_call(
        kernel,
        out_shape=jax.ShapeDtypeStruct((2 * half, hid), owns[0].dtype),
        in_specs=[SMEM, SMEM] + [VMEM] * (2 * CHUNKS + X),
        out_specs=VMEM,
        scratch_shapes=[pltpu.VMEM((half, hid), jnp.float32)],
        name="heads_grad",
    )(at.reshape(1), jnp.stack([r for group in rows for r in group]), *owns, *oths, *weights)


def sum_first(parts):
    hid = parts.shape[1]
    rows = hid // Y

    def kernel(src, out):
        for y in range(Y):
            for col in range(ZH):
                v = src[:, y * rows:(y + 1) * rows, col * LANE:(col + 1) * LANE].astype(jnp.float32)
                out[y, col] = jnp.sum(v, axis=0).astype(out.dtype)

    return pl.pallas_call(
        kernel,
        out_shape=jax.ShapeDtypeStruct((Y, ZH, rows, LANE), parts.dtype),
        in_specs=[VMEM],
        out_specs=VMEM,
        name="sum_first",
    )(parts)


def sum_second(parts, first):
    hid = parts[0].shape[0]
    rows = hid // Y

    def kernel(*refs):
        before, out = refs[-2:]
        for y in range(Y):
            for col in range(ZH):
                total = None
                for ref in refs[:-2]:
                    v = ref[y * rows:(y + 1) * rows, col * LANE:(col + 1) * LANE].astype(jnp.float32)
                    total = v if total is None else total + v
                out[y, col, 0] = before[y, col]
                out[y, col, 1] = total.astype(out.dtype)

    return pl.pallas_call(
        kernel,
        out_shape=jax.ShapeDtypeStruct((Y, ZH, CHUNKS, rows, LANE), parts[0].dtype),
        in_specs=[VMEM] * (X + 1),
        out_specs=VMEM,
        name="sum_second",
    )(*parts, first)


def spread_sum(parts):
    shape = (Y,) + parts.shape[1:]

    def kernel(src, out):
        total = jnp.sum(src[...].astype(jnp.float32), axis=0).astype(out.dtype)
        for y in range(Y):
            out[y] = total

    return pl.pallas_call(
        kernel,
        out_shape=jax.ShapeDtypeStruct(shape, parts.dtype),
        in_specs=[VMEM],
        out_specs=VMEM,
        name="spread_sum",
    )(parts)


def spread_rows(parts):
    rows = parts.shape[2]

    def kernel(src, out):
        for x in range(X):
            for y in range(Y):
                for h in range(CHUNKS):
                    out[x, h, y * rows:(y + 1) * rows] = src[y, h]

    return pl.pallas_call(
        kernel,
        out_shape=jax.ShapeDtypeStruct((X, CHUNKS, Y * rows, LANE), parts.dtype),
        in_specs=[VMEM],
        out_specs=VMEM,
        name="spread_rows",
    )(parts)


def finish(parts, scale):
    hid = parts.shape[2]
    rows = hid // 2

    def kernel(src, out):
        for h in range(CHUNKS):
            for x in range(X):
                at = (h * X + x) * LANE
                out[:, at:at + LANE] = src[x, h].astype(jnp.float32) * scale

    return pl.pallas_call(
        kernel,
        grid=(2,),
        out_shape=jax.ShapeDtypeStruct((hid, CHUNKS * X * LANE), jnp.float32),
        in_specs=[pl.BlockSpec((X, CHUNKS, rows, LANE), lambda i: (0, 0, i, 0))],
        out_specs=pl.BlockSpec((rows, CHUNKS * X * LANE), lambda i: (i, 0)),
        name="finish",
    )(parts)


def per_device(heads, weight, cot):
    xi, yi = lax.axis_index("x"), lax.axis_index("y")
    zl, core, zh = lax.axis_index("zl"), lax.axis_index("core"), lax.axis_index("zh")
    tok, feat = cot.shape
    hid = weight.shape[0]
    blk = tok // ZH
    grad_scale = float(heads.shape[0] * ZH * Y * X) ** (-0.5)

    def order(m, c):
        return (m % ZL) * CORE + c

    rows = [[order(zl, c), order(zl + 2, c), order(zl + 1, c)] for c in (core, 1 - core)]

    sends = [lax.dynamic_slice(cot, ((zh + k) % ZH * blk, 0), (blk, feat)) for k in range(ZH)]
    got = [lax.ppermute(sends[k], ("zl", "core", "zh"), spread_pairs(k)) for k in range(ZH)]

    wr, wc = hid // Y, feat // X
    w_part = lax.dynamic_slice(weight, (yi * wr, xi * wc), (wr, wc))
    w_far = [lax.ppermute(w_part, "zh", ring(ZH, k)) for k in range(1, ZH)]
    w_y = spread_cols([w_part] + w_far, zh)
    w_y = lax.all_to_all(w_y, "y", 0, 0)
    w_y = weight_rows(w_y)
    w_x = [w_y] + [lax.ppermute(w_y, "x", ring(X, k)) for k in range(1, X)]

    heads_t = order_heads(heads, rows)

    mine = gather_tokens(got, (zh * ROW + zl * CORE + core) % ZH)
    near = []
    for h in range(CHUNKS):
        near.append([mine[h]] + [lax.ppermute(mine[h], "zl", ring(ZL, k)) for k in (1, 2)])
    owns, oths = [], []
    for h in range(CHUNKS):
        own = jnp.concatenate(near[h], axis=0)
        oth = lax.ppermute(own, "core", ring(CORE, 1))
        owns.append(own)
        oths.append(oth)
    part = weight_stack(heads_t, owns[0], oths[0])
    part = lax.all_to_all(part, "x", 0, 0)
    first = sum_first(part)
    part = weight_part(heads_t, owns[1], oths[1], xi)
    part = [part[0]] + [lax.ppermute(part[k], "x", ring(X, k)) for k in range(1, X)]
    r = sum_second(part, first)
    r = lax.all_to_all(r.reshape((Y * ZH,) + r.shape[2:]), ("y", "zh"), 0, 0)
    r = spread_sum(r)
    r = lax.all_to_all(r, "y", 0, 0)
    r = spread_rows(r)
    r = lax.all_to_all(r, "x", 0, 0)
    weight_grad = finish(r, grad_scale)

    head_grad = heads_grad(owns, oths, w_x, rows, xi)
    return head_grad, weight_grad


def solution(mesh):
    fine = Mesh(mesh.devices.reshape(Y, X, ZL, CORE, ZH), ("y", "x", "zl", "core", "zh"))

    return jax.shard_map(
        per_device,
        mesh=fine,
        in_specs=(P(("y", "x", "zh"), ("zl", "core")), P(("zl", "core"), "zh"), P(("y", "x", "zl", "core"), "zh")),
        out_specs=(P(("y", "x", "zh"), ("zl", "core")), P(("zl", "core"), "zh")),
        check_vma=False,
    )
```

```python
import jax
import jax.numpy as jnp
from jax import lax
from jax.experimental import pallas as pl
from jax.experimental.pallas import tpu as pltpu
from jax.sharding import Mesh, PartitionSpec as P


Y, X, ZL, CORE, ZH = 8, 4, 3, 2, 4
ROW = ZL * CORE
CHUNKS = 2
LANE = 128
XS = 4


SMEM = pl.BlockSpec(memory_space=pltpu.SMEM)
VMEM = pl.BlockSpec(memory_space=pltpu.VMEM)


def ring(n, step):
    return [(i, (i + step) % n) for i in range(n)]


def spread_pairs(k):
    pairs = []
    for row in range(ROW):
        for col in range(ZH):
            d = ZH * row + (col + k) % ZH
            pairs.append((row * ZH + col, (d % ROW) * ZH + d // ROW))
    return pairs


def gather_tokens(got, at):
    blk, feat = got[0].shape
    n = feat // CHUNKS

    def kernel(at_ref, *refs):
        outs = refs[ZH:]
        for col in range(ZH):
            k = (at_ref[0] + (ZH - col)) % ZH
            for i in range(ZH):

                @pl.when(k == i)
                def _():
                    for h in range(CHUNKS):
                        for s in range(XS):
                            fro = h * n + s * LANE
                            outs[h][s, :, col * LANE:(col + 1) * LANE] = refs[i][:, fro:fro + LANE]

    return pl.pallas_call(
        kernel,
        out_shape=[jax.ShapeDtypeStruct((XS, blk, ZH * LANE), got[0].dtype)] * CHUNKS,
        in_specs=[SMEM] + [VMEM] * ZH,
        out_specs=[VMEM] * CHUNKS,
        name="gather_tokens",
    )(at.reshape(1), *got)


def order_heads(pieces, rows, at):
    tok, hid = pieces[0].shape
    n = len(rows[0])
    blk = tok // ROW

    def kernel(at_ref, rows_ref, *refs):
        outs = refs[X:]
        for k in range(X):
            x = (at_ref[0] + (X - k)) % X
            for o, out in enumerate(outs):
                for i in range(n):
                    fro = pl.multiple_of(rows_ref[o * n + i] * blk, blk)
                    to = pl.multiple_of((i * X + x) * blk, blk)
                    out[:, pl.ds(to, blk)] = refs[k][pl.ds(fro, blk), :].T

    return pl.pallas_call(
        kernel,
        out_shape=[jax.ShapeDtypeStruct((hid, n * X * blk), pieces[0].dtype)] * len(rows),
        in_specs=[SMEM, SMEM] + [VMEM] * X,
        out_specs=[VMEM] * len(rows),
        name="order_heads",
    )(at.reshape(1), jnp.stack([r for group in rows for r in group]), *pieces)


def spread_cols(pieces, at):
    shape = pieces[0].shape

    def kernel(at_ref, *refs):
        out = refs[-1]
        for col in range(ZH):
            k = (at_ref[0] + (ZH - col)) % ZH
            for i in range(ZH):

                @pl.when(k == i)
                def _():
                    v = refs[i][...]
                    for y in range(Y):
                        out[y, col] = v

    return pl.pallas_call(
        kernel,
        out_shape=jax.ShapeDtypeStruct((Y, ZH) + shape, pieces[0].dtype),
        in_specs=[SMEM] + [VMEM] * ZH,
        out_specs=VMEM,
        name="spread_cols",
    )(at.reshape(1), *pieces)


def weight_rows(pieces):
    _, _, rows, wc = pieces.shape

    def kernel(src, out):
        for y in range(Y):
            for col in range(ZH):
                for s in range(wc // LANE):
                    to = (s * ZH + col) * LANE
                    out[y * rows:(y + 1) * rows, to:to + LANE] = src[y, col, :, s * LANE:(s + 1) * LANE]

    return pl.pallas_call(
        kernel,
        out_shape=jax.ShapeDtypeStruct((Y * rows, ZH * wc), pieces.dtype),
        in_specs=[VMEM],
        out_specs=VMEM,
        name="weight_rows",
    )(pieces)


def weight_part(heads_t, own, oth):
    hid = heads_t[0].shape[0]
    rows = hid // Y

    def kernel(a, b, c, d, out):
        acc = jnp.dot(a[...], c[...], preferred_element_type=jnp.float32)
        acc += jnp.dot(b[...], d[...], preferred_element_type=jnp.float32)
        acc = acc.astype(out.dtype)
        for y in range(Y):
            for col in range(ZH):
                out[y, col] = acc[y * rows:(y + 1) * rows, col * LANE:(col + 1) * LANE]

    return pl.pallas_call(
        kernel,
        out_shape=jax.ShapeDtypeStruct((Y, ZH, rows, LANE), own.dtype),
        in_specs=[VMEM] * 4,
        out_specs=VMEM,
        name="weight_part",
    )(*heads_t, own, oth)


def heads_part(owns, oths, weight, rows, at):
    hid, feat = weight.shape
    n = feat // CHUNKS
    count = len(rows[0])
    blk = owns[0].shape[0] // (count * X)

    def kernel(at_ref, rows_ref, *refs):
        sides = (refs[:CHUNKS], refs[CHUNKS:2 * CHUNKS])
        w_ref, outs = refs[2 * CHUNKS], refs[2 * CHUNKS + 1:]
        for k in range(X):
            x = (at_ref[0] + k) % X
            for o, side in enumerate(sides):
                for i in range(count):
                    fro = pl.multiple_of((i * X + x) * blk, blk)
                    acc = None
                    for h in range(CHUNKS):
                        prod = lax.dot_general(
                            side[h][pl.ds(fro, blk), :], w_ref[:, h * n:(h + 1) * n], (((1,), (1,)), ((), ())),
                            preferred_element_type=jnp.float32,
                        )
                        acc = prod if acc is None else acc + prod
                    to = pl.multiple_of(rows_ref[o * count + i] * blk, blk)
                    outs[k][pl.ds(to, blk), :] = acc.astype(weight.dtype)

    return pl.pallas_call(
        kernel,
        out_shape=[jax.ShapeDtypeStruct((2 * count * blk, hid), weight.dtype)] * X,
        in_specs=[SMEM, SMEM] + [VMEM] * (2 * CHUNKS + 1),
        out_specs=[VMEM] * X,
        name="heads_part",
    )(at.reshape(1), jnp.stack([r for group in rows for r in group]), *owns, *oths, weight)


def heads_sum(parts):
    def kernel(*refs):
        total = None
        for ref in refs[:-1]:
            v = ref[...].astype(jnp.float32)
            total = v if total is None else total + v
        refs[-1][...] = total.astype(refs[-1].dtype)

    tok, hid = parts[0].shape
    spec = pl.BlockSpec((tok // 4, hid), lambda i: (i, 0))
    return pl.pallas_call(
        kernel,
        grid=(4,),
        out_shape=jax.ShapeDtypeStruct((tok, hid), parts[0].dtype),
        in_specs=[spec] * len(parts),
        out_specs=spec,
        name="heads_sum",
    )(*parts)


def sum_rows(parts):
    _, _, rows, _ = parts[0].shape

    def kernel(*refs):
        out = refs[-1]
        for h in range(CHUNKS):
            for col in range(ZH):
                out[col, h] = jnp.sum(refs[h][:, col].astype(jnp.float32), axis=0).astype(out.dtype)

    return pl.pallas_call(
        kernel,
        out_shape=jax.ShapeDtypeStruct((ZH, CHUNKS, rows, LANE), parts[0].dtype),
        in_specs=[VMEM] * CHUNKS,
        out_specs=VMEM,
        name="sum_rows",
    )(*parts)


def spread_sum(parts):
    shape = (Y,) + parts.shape[1:]

    def kernel(src, out):
        total = jnp.sum(src[...].astype(jnp.float32), axis=0).astype(out.dtype)
        for y in range(Y):
            out[y] = total

    return pl.pallas_call(
        kernel,
        out_shape=jax.ShapeDtypeStruct(shape, parts.dtype),
        in_specs=[VMEM],
        out_specs=VMEM,
        name="spread_sum",
    )(parts)


def spread_rows(parts):
    rows = parts.shape[2]

    def kernel(src, out):
        for x in range(X):
            for y in range(Y):
                for h in range(CHUNKS):
                    out[x, h, y * rows:(y + 1) * rows] = src[y, h]

    return pl.pallas_call(
        kernel,
        out_shape=jax.ShapeDtypeStruct((X, CHUNKS, Y * rows, LANE), parts.dtype),
        in_specs=[VMEM],
        out_specs=VMEM,
        name="spread_rows",
    )(parts)


def finish(parts, scale):
    hid = parts.shape[2]
    rows = hid // 2

    def kernel(src, out):
        for h in range(CHUNKS):
            for x in range(X):
                at = (h * X + x) * LANE
                out[:, at:at + LANE] = src[x, h].astype(jnp.float32) * scale

    return pl.pallas_call(
        kernel,
        grid=(2,),
        out_shape=jax.ShapeDtypeStruct((hid, CHUNKS * X * LANE), jnp.float32),
        in_specs=[pl.BlockSpec((X, CHUNKS, rows, LANE), lambda i: (0, 0, i, 0))],
        out_specs=pl.BlockSpec((rows, CHUNKS * X * LANE), lambda i: (i, 0)),
        name="finish",
    )(parts)


def per_device(heads, weight, cot):
    xi, yi = lax.axis_index("x"), lax.axis_index("y")
    zl, core, zh = lax.axis_index("zl"), lax.axis_index("core"), lax.axis_index("zh")
    tok, feat = cot.shape
    hid = weight.shape[0]
    blk = tok // ZH
    grad_scale = float(heads.shape[0] * ZH * Y * X) ** (-0.5)

    def order(m, c):
        return (m % ZL) * CORE + c

    rows = [[order(zl, c), order(zl + 2, c), order(zl + 1, c)] for c in (core, 1 - core)]

    sends = [lax.dynamic_slice(cot, ((zh + k) % ZH * blk, 0), (blk, feat)) for k in range(ZH)]
    got = [lax.ppermute(sends[k], ("zl", "core", "zh"), spread_pairs(k)) for k in range(ZH)]

    heads_x = [heads] + [lax.ppermute(heads, "x", ring(X, k)) for k in range(1, X)]
    heads_t = order_heads(heads_x, rows, xi)

    mine = gather_tokens(got, (zh * ROW + zl * CORE + core) % ZH)
    near = []
    for h in range(CHUNKS):
        part = lax.all_to_all(mine[h], "x", 0, 0)
        part = part.reshape(X * blk, ZH * LANE)
        near.append([part] + [lax.ppermute(part, "zl", ring(ZL, k)) for k in (1, 2)])

    wr = hid // Y
    w_part = jnp.concatenate(
        [lax.dynamic_slice(weight, (yi * wr, (h * X + xi) * LANE), (wr, LANE)) for h in range(CHUNKS)], axis=1
    )
    w_far = [lax.ppermute(w_part, "zh", ring(ZH, k)) for k in range(1, ZH)]
    w_y = spread_cols([w_part] + w_far, zh)
    w_y = lax.all_to_all(w_y, "y", 0, 0)
    w_y = weight_rows(w_y)

    owns, oths, parts = [], [], []
    for h in range(CHUNKS):
        own = jnp.concatenate(near[h], axis=0)
        oth = lax.ppermute(own, "core", ring(CORE, 1))
        owns.append(own)
        oths.append(oth)
        part = weight_part(heads_t, own, oth)
        parts.append(lax.all_to_all(part, "y", 0, 0))
    r = sum_rows(parts)
    r = lax.all_to_all(r, "zh", 0, 0)
    r = spread_sum(r)
    r = lax.all_to_all(r, "y", 0, 0)
    r = spread_rows(r)
    r = lax.all_to_all(r, "x", 0, 0)
    weight_grad = finish(r, grad_scale)

    part = heads_part(owns, oths, w_y, rows, xi)
    part = [part[0]] + [lax.ppermute(part[k], "x", ring(X, k)) for k in range(1, X)]
    head_grad = heads_sum(part)
    return head_grad, weight_grad


def solution(mesh):
    fine = Mesh(mesh.devices.reshape(Y, X, ZL, CORE, ZH), ("y", "x", "zl", "core", "zh"))

    return jax.shard_map(
        per_device,
        mesh=fine,
        in_specs=(P(("y", "x", "zh"), ("zl", "core")), P(("zl", "core"), "zh"), P(("y", "x", "zl", "core"), "zh")),
        out_specs=(P(("y", "x", "zh"), ("zl", "core")), P(("zl", "core"), "zh")),
        check_vma=False,
    )
```

```python
import jax
import jax.numpy as jnp
from jax import lax
from jax.experimental import pallas as pl
from jax.experimental.pallas import tpu as pltpu
from jax.sharding import Mesh, PartitionSpec as P


Y, X, ZL, CORE, ZH = 8, 4, 3, 2, 4
ROW = ZL * CORE
CHUNKS = 2
LANE = 128
XS = 4


SMEM = pl.BlockSpec(memory_space=pltpu.SMEM)
VMEM = pl.BlockSpec(memory_space=pltpu.VMEM)


def ring(n, step):
    return [(i, (i + step) % n) for i in range(n)]


def spread_pairs(k):
    pairs = []
    for row in range(ROW):
        for col in range(ZH):
            d = ZH * row + (col + k) % ZH
            pairs.append((row * ZH + col, (d % ROW) * ZH + d // ROW))
    return pairs


def gather_tokens(got, at):
    blk, feat = got[0].shape
    n = feat // CHUNKS

    def kernel(at_ref, *refs):
        outs = refs[ZH:]
        for col in range(ZH):
            k = (at_ref[0] + (ZH - col)) % ZH
            for i in range(ZH):

                @pl.when(k == i)
                def _():
                    for h in range(CHUNKS):
                        for s in range(XS):
                            fro = h * n + s * LANE
                            outs[h][s, :, col * LANE:(col + 1) * LANE] = refs[i][:, fro:fro + LANE]

    return pl.pallas_call(
        kernel,
        out_shape=[jax.ShapeDtypeStruct((XS, blk, ZH * LANE), got[0].dtype)] * CHUNKS,
        in_specs=[SMEM] + [VMEM] * ZH,
        out_specs=[VMEM] * CHUNKS,
        name="gather_tokens",
    )(at.reshape(1), *got)


def order_heads(pieces, rows, at):
    tok, hid = pieces[0].shape
    n = len(rows[0])
    blk = tok // ROW

    def kernel(at_ref, rows_ref, *refs):
        outs = refs[X:]
        for k in range(X):
            x = (at_ref[0] + (X - k)) % X
            for o, out in enumerate(outs):
                for i in range(n):
                    fro = pl.multiple_of(rows_ref[o * n + i] * blk, blk)
                    to = pl.multiple_of((i * X + x) * blk, blk)
                    out[:, pl.ds(to, blk)] = refs[k][pl.ds(fro, blk), :].T

    return pl.pallas_call(
        kernel,
        out_shape=[jax.ShapeDtypeStruct((hid, n * X * blk), pieces[0].dtype)] * len(rows),
        in_specs=[SMEM, SMEM] + [VMEM] * X,
        out_specs=[VMEM] * len(rows),
        name="order_heads",
    )(at.reshape(1), jnp.stack([r for group in rows for r in group]), *pieces)


def spread_cols(pieces, at):
    shape = pieces[0].shape

    def kernel(at_ref, *refs):
        out = refs[-1]
        for col in range(ZH):
            k = (at_ref[0] + (ZH - col)) % ZH
            for i in range(ZH):

                @pl.when(k == i)
                def _():
                    v = refs[i][...]
                    for y in range(Y):
                        out[y, col] = v

    return pl.pallas_call(
        kernel,
        out_shape=jax.ShapeDtypeStruct((Y, ZH) + shape, pieces[0].dtype),
        in_specs=[SMEM] + [VMEM] * ZH,
        out_specs=VMEM,
        name="spread_cols",
    )(at.reshape(1), *pieces)


def weight_rows(pieces):
    _, _, rows, wc = pieces.shape

    def kernel(src, out):
        for y in range(Y):
            for col in range(ZH):
                for s in range(wc // LANE):
                    to = (s * ZH + col) * LANE
                    out[y * rows:(y + 1) * rows, to:to + LANE] = src[y, col, :, s * LANE:(s + 1) * LANE]

    return pl.pallas_call(
        kernel,
        out_shape=jax.ShapeDtypeStruct((Y * rows, ZH * wc), pieces.dtype),
        in_specs=[VMEM],
        out_specs=VMEM,
        name="weight_rows",
    )(pieces)


def weight_part(heads_t, own, oth, before=None):
    hid = heads_t[0].shape[0]
    rows = hid // Y
    both = before is not None

    def kernel(a, b, c, d, *refs):
        out = refs[-1]
        acc = jnp.dot(a[...], c[...], preferred_element_type=jnp.float32)
        acc += jnp.dot(b[...], d[...], preferred_element_type=jnp.float32)
        acc = acc.astype(out.dtype)
        for y in range(Y):
            for col in range(ZH):
                v = acc[y * rows:(y + 1) * rows, col * LANE:(col + 1) * LANE]
                if both:
                    out[y, col, 0] = refs[0][y, col]
                    out[y, col, 1] = v
                else:
                    out[y, col] = v

    shape = (Y, ZH, CHUNKS, rows, LANE) if both else (Y, ZH, rows, LANE)
    return pl.pallas_call(
        kernel,
        out_shape=jax.ShapeDtypeStruct(shape, own.dtype),
        in_specs=[VMEM] * (5 if both else 4),
        out_specs=VMEM,
        name="weight_part",
    )(*heads_t, own, oth, *((before,) if both else ()))


def heads_part(owns, oths, weight, rows, at):
    hid, feat = weight.shape
    n = feat // CHUNKS
    count = len(rows[0])
    blk = owns[0].shape[0] // (count * X)

    def kernel(at_ref, rows_ref, *refs):
        sides = (refs[:CHUNKS], refs[CHUNKS:2 * CHUNKS])
        w_ref, outs = refs[2 * CHUNKS], refs[2 * CHUNKS + 1:]
        for k in range(X):
            x = (at_ref[0] + k) % X
            for o, side in enumerate(sides):
                for i in range(count):
                    fro = pl.multiple_of((i * X + x) * blk, blk)
                    acc = None
                    for h in range(CHUNKS):
                        prod = lax.dot_general(
                            side[h][pl.ds(fro, blk), :], w_ref[:, h * n:(h + 1) * n], (((1,), (1,)), ((), ())),
                            preferred_element_type=jnp.float32,
                        )
                        acc = prod if acc is None else acc + prod
                    to = pl.multiple_of(rows_ref[o * count + i] * blk, blk)
                    outs[k][pl.ds(to, blk), :] = acc.astype(weight.dtype)

    return pl.pallas_call(
        kernel,
        out_shape=[jax.ShapeDtypeStruct((2 * count * blk, hid), weight.dtype)] * X,
        in_specs=[SMEM, SMEM] + [VMEM] * (2 * CHUNKS + 1),
        out_specs=[VMEM] * X,
        name="heads_part",
    )(at.reshape(1), jnp.stack([r for group in rows for r in group]), *owns, *oths, weight)


def heads_sum(parts):
    def kernel(*refs):
        total = None
        for ref in refs[:-1]:
            v = ref[...].astype(jnp.float32)
            total = v if total is None else total + v
        refs[-1][...] = total.astype(refs[-1].dtype)

    tok, hid = parts[0].shape
    spec = pl.BlockSpec((tok // 4, hid), lambda i: (i, 0))
    return pl.pallas_call(
        kernel,
        grid=(4,),
        out_shape=jax.ShapeDtypeStruct((tok, hid), parts[0].dtype),
        in_specs=[spec] * len(parts),
        out_specs=spec,
        name="heads_sum",
    )(*parts)


def sum_rows(parts):
    def kernel(src, out):
        for col in range(ZH):
            out[col] = jnp.sum(src[:, col].astype(jnp.float32), axis=0).astype(out.dtype)

    return pl.pallas_call(
        kernel,
        out_shape=jax.ShapeDtypeStruct(parts.shape[1:], parts.dtype),
        in_specs=[VMEM],
        out_specs=VMEM,
        name="sum_rows",
    )(parts)


def spread_sum(parts):
    shape = (Y,) + parts.shape[1:]

    def kernel(src, out):
        total = jnp.sum(src[...].astype(jnp.float32), axis=0).astype(out.dtype)
        for y in range(Y):
            out[y] = total

    return pl.pallas_call(
        kernel,
        out_shape=jax.ShapeDtypeStruct(shape, parts.dtype),
        in_specs=[VMEM],
        out_specs=VMEM,
        name="spread_sum",
    )(parts)


def spread_rows(parts):
    rows = parts.shape[2]

    def kernel(src, out):
        for x in range(X):
            for y in range(Y):
                for h in range(CHUNKS):
                    out[x, h, y * rows:(y + 1) * rows] = src[y, h]

    return pl.pallas_call(
        kernel,
        out_shape=jax.ShapeDtypeStruct((X, CHUNKS, Y * rows, LANE), parts.dtype),
        in_specs=[VMEM],
        out_specs=VMEM,
        name="spread_rows",
    )(parts)


def finish(parts, scale):
    hid = parts.shape[2]
    rows = hid // 2

    def kernel(src, out):
        for h in range(CHUNKS):
            for x in range(X):
                at = (h * X + x) * LANE
                out[:, at:at + LANE] = src[x, h].astype(jnp.float32) * scale

    return pl.pallas_call(
        kernel,
        grid=(2,),
        out_shape=jax.ShapeDtypeStruct((hid, CHUNKS * X * LANE), jnp.float32),
        in_specs=[pl.BlockSpec((X, CHUNKS, rows, LANE), lambda i: (0, 0, i, 0))],
        out_specs=pl.BlockSpec((rows, CHUNKS * X * LANE), lambda i: (i, 0)),
        name="finish",
    )(parts)


def per_device(heads, weight, cot):
    xi, yi = lax.axis_index("x"), lax.axis_index("y")
    zl, core, zh = lax.axis_index("zl"), lax.axis_index("core"), lax.axis_index("zh")
    tok, feat = cot.shape
    hid = weight.shape[0]
    blk = tok // ZH
    grad_scale = float(heads.shape[0] * ZH * Y * X) ** (-0.5)

    def order(m, c):
        return (m % ZL) * CORE + c

    rows = [[order(zl, c), order(zl + 2, c), order(zl + 1, c)] for c in (core, 1 - core)]

    sends = [lax.dynamic_slice(cot, ((zh + k) % ZH * blk, 0), (blk, feat)) for k in range(ZH)]
    got = [lax.ppermute(sends[k], ("zl", "core", "zh"), spread_pairs(k)) for k in range(ZH)]

    heads_x = [heads] + [lax.ppermute(heads, "x", ring(X, k)) for k in range(1, X)]
    heads_t = order_heads(heads_x, rows, xi)

    mine = gather_tokens(got, (zh * ROW + zl * CORE + core) % ZH)
    near = []
    for h in range(CHUNKS):
        part = lax.all_to_all(mine[h], "x", 0, 0)
        part = part.reshape(X * blk, ZH * LANE)
        near.append([part] + [lax.ppermute(part, "zl", ring(ZL, k)) for k in (1, 2)])

    wr = hid // Y
    w_part = jnp.concatenate(
        [lax.dynamic_slice(weight, (yi * wr, (h * X + xi) * LANE), (wr, LANE)) for h in range(CHUNKS)], axis=1
    )
    w_far = [lax.ppermute(w_part, "zh", ring(ZH, k)) for k in range(1, ZH)]
    w_y = spread_cols([w_part] + w_far, zh)
    w_y = lax.all_to_all(w_y, "y", 0, 0)
    w_y = weight_rows(w_y)

    owns, oths = [], []
    for h in range(CHUNKS):
        own = jnp.concatenate(near[h], axis=0)
        oth = lax.ppermute(own, "core", ring(CORE, 1))
        owns.append(own)
        oths.append(oth)
    first = weight_part(heads_t, owns[0], oths[0])
    r = weight_part(heads_t, owns[1], oths[1], first)
    r = lax.all_to_all(r, "y", 0, 0)
    r = sum_rows(r)
    r = lax.all_to_all(r, "zh", 0, 0)
    r = spread_sum(r)
    r = lax.all_to_all(r, "y", 0, 0)
    r = spread_rows(r)
    r = lax.all_to_all(r, "x", 0, 0)
    weight_grad = finish(r, grad_scale)

    part = heads_part(owns, oths, w_y, rows, xi)
    part = [part[0]] + [lax.ppermute(part[k], "x", ring(X, k)) for k in range(1, X)]
    head_grad = heads_sum(part)
    return head_grad, weight_grad


def solution(mesh):
    fine = Mesh(mesh.devices.reshape(Y, X, ZL, CORE, ZH), ("y", "x", "zl", "core", "zh"))

    return jax.shard_map(
        per_device,
        mesh=fine,
        in_specs=(P(("y", "x", "zh"), ("zl", "core")), P(("zl", "core"), "zh"), P(("y", "x", "zl", "core"), "zh")),
        out_specs=(P(("y", "x", "zh"), ("zl", "core")), P(("zl", "core"), "zh")),
        check_vma=False,
    )
```

```python
import jax
import jax.numpy as jnp
from jax import lax
from jax.experimental import pallas as pl
from jax.experimental.pallas import tpu as pltpu
from jax.sharding import Mesh, PartitionSpec as P


Y, X, ZL, CORE, ZH = 8, 4, 3, 2, 4
ROW = ZL * CORE
CHUNKS = 2
LANE = 128
XS = 4


SMEM = pl.BlockSpec(memory_space=pltpu.SMEM)
VMEM = pl.BlockSpec(memory_space=pltpu.VMEM)


def ring(n, step):
    return [(i, (i + step) % n) for i in range(n)]


def spread_pairs(k):
    pairs = []
    for row in range(ROW):
        for col in range(ZH):
            d = ZH * row + (col + k) % ZH
            pairs.append((row * ZH + col, (d % ROW) * ZH + d // ROW))
    return pairs


def gather_tokens(got, at):
    blk, feat = got[0].shape
    n = feat // CHUNKS

    def kernel(at_ref, *refs):
        outs = refs[ZH:]
        for col in range(ZH):
            k = (at_ref[0] + (ZH - col)) % ZH
            for i in range(ZH):

                @pl.when(k == i)
                def _():
                    for h in range(CHUNKS):
                        for s in range(XS):
                            fro = h * n + s * LANE
                            outs[h][s, :, col * LANE:(col + 1) * LANE] = refs[i][:, fro:fro + LANE]

    return pl.pallas_call(
        kernel,
        out_shape=[jax.ShapeDtypeStruct((XS, blk, ZH * LANE), got[0].dtype)] * CHUNKS,
        in_specs=[SMEM] + [VMEM] * ZH,
        out_specs=[VMEM] * CHUNKS,
        name="gather_tokens",
    )(at.reshape(1), *got)


def order_heads(pieces, rows, at):
    tok, hid = pieces[0].shape
    n = len(rows[0])
    blk = tok // ROW

    def kernel(at_ref, rows_ref, *refs):
        outs = refs[X:]
        for k in range(X):
            x = (at_ref[0] + (X - k)) % X
            for o, out in enumerate(outs):
                for i in range(n):
                    fro = pl.multiple_of(rows_ref[o * n + i] * blk, blk)
                    to = pl.multiple_of((i * X + x) * blk, blk)
                    out[:, pl.ds(to, blk)] = refs[k][pl.ds(fro, blk), :].T

    return pl.pallas_call(
        kernel,
        out_shape=[jax.ShapeDtypeStruct((hid, n * X * blk), pieces[0].dtype)] * len(rows),
        in_specs=[SMEM, SMEM] + [VMEM] * X,
        out_specs=[VMEM] * len(rows),
        name="order_heads",
    )(at.reshape(1), jnp.stack([r for group in rows for r in group]), *pieces)


def spread_cols(pieces, at):
    shape = pieces[0].shape

    def kernel(at_ref, *refs):
        out = refs[-1]
        for col in range(ZH):
            k = (at_ref[0] + (ZH - col)) % ZH
            for i in range(ZH):

                @pl.when(k == i)
                def _():
                    v = refs[i][...]
                    for y in range(Y):
                        out[y, col] = v

    return pl.pallas_call(
        kernel,
        out_shape=jax.ShapeDtypeStruct((Y, ZH) + shape, pieces[0].dtype),
        in_specs=[SMEM] + [VMEM] * ZH,
        out_specs=VMEM,
        name="spread_cols",
    )(at.reshape(1), *pieces)


def weight_rows(pieces):
    _, _, rows, wc = pieces.shape

    def kernel(src, out):
        for y in range(Y):
            for col in range(ZH):
                for s in range(wc // LANE):
                    to = (s * ZH + col) * LANE
                    out[y * rows:(y + 1) * rows, to:to + LANE] = src[y, col, :, s * LANE:(s + 1) * LANE]

    return pl.pallas_call(
        kernel,
        out_shape=jax.ShapeDtypeStruct((Y * rows, ZH * wc), pieces.dtype),
        in_specs=[VMEM],
        out_specs=VMEM,
        name="weight_rows",
    )(pieces)


def weight_part(heads_t, own, oth, before=None):
    hid = heads_t[0].shape[0]
    rows = hid // Y
    both = before is not None

    def kernel(a, b, c, d, *refs):
        out = refs[-1]
        acc = jnp.dot(a[...], c[...], preferred_element_type=jnp.float32)
        acc += jnp.dot(b[...], d[...], preferred_element_type=jnp.float32)
        acc = acc.astype(out.dtype)
        for y in range(Y):
            for col in range(ZH):
                v = acc[y * rows:(y + 1) * rows, col * LANE:(col + 1) * LANE]
                if both:
                    out[y, col, 0] = refs[0][y, col]
                    out[y, col, 1] = v
                else:
                    out[y, col] = v

    shape = (Y, ZH, CHUNKS, rows, LANE) if both else (Y, ZH, rows, LANE)
    return pl.pallas_call(
        kernel,
        out_shape=jax.ShapeDtypeStruct(shape, own.dtype),
        in_specs=[VMEM] * (5 if both else 4),
        out_specs=VMEM,
        name="weight_part",
    )(*heads_t, own, oth, *((before,) if both else ()))


def heads_part(owns, oths, weight, rows, at):
    hid, feat = weight.shape
    n = feat // CHUNKS
    count = len(rows[0])
    blk = owns[0].shape[0] // (count * X)

    def kernel(at_ref, rows_ref, *refs):
        sides = (refs[:CHUNKS], refs[CHUNKS:2 * CHUNKS])
        w_ref, outs = refs[2 * CHUNKS], refs[2 * CHUNKS + 1:]
        for k in range(X):
            x = (at_ref[0] + k) % X
            for o, side in enumerate(sides):
                for i in range(count):
                    fro = pl.multiple_of((i * X + x) * blk, blk)
                    acc = None
                    for h in range(CHUNKS):
                        prod = lax.dot_general(
                            side[h][pl.ds(fro, blk), :], w_ref[:, h * n:(h + 1) * n], (((1,), (1,)), ((), ())),
                            preferred_element_type=jnp.float32,
                        )
                        acc = prod if acc is None else acc + prod
                    to = pl.multiple_of(rows_ref[o * count + i] * blk, blk)
                    outs[k][pl.ds(to, blk), :] = acc.astype(weight.dtype)

    return pl.pallas_call(
        kernel,
        out_shape=[jax.ShapeDtypeStruct((2 * count * blk, hid), weight.dtype)] * X,
        in_specs=[SMEM, SMEM] + [VMEM] * (2 * CHUNKS + 1),
        out_specs=[VMEM] * X,
        name="heads_part",
    )(at.reshape(1), jnp.stack([r for group in rows for r in group]), *owns, *oths, weight)


def heads_sum(parts):
    def kernel(*refs):
        total = None
        for ref in refs[:-1]:
            v = ref[...].astype(jnp.float32)
            total = v if total is None else total + v
        refs[-1][...] = total.astype(refs[-1].dtype)

    tok, hid = parts[0].shape
    spec = pl.BlockSpec((tok // 4, hid), lambda i: (i, 0))
    return pl.pallas_call(
        kernel,
        grid=(4,),
        out_shape=jax.ShapeDtypeStruct((tok, hid), parts[0].dtype),
        in_specs=[spec] * len(parts),
        out_specs=spec,
        name="heads_sum",
    )(*parts)


def spread_sum(parts):
    shape = (Y,) + parts.shape[1:]

    def kernel(src, out):
        total = jnp.sum(src[...].astype(jnp.float32), axis=0).astype(out.dtype)
        for y in range(Y):
            out[y] = total

    return pl.pallas_call(
        kernel,
        out_shape=jax.ShapeDtypeStruct(shape, parts.dtype),
        in_specs=[VMEM],
        out_specs=VMEM,
        name="spread_sum",
    )(parts)


def spread_rows(parts):
    rows = parts.shape[2]

    def kernel(src, out):
        for x in range(X):
            for y in range(Y):
                for h in range(CHUNKS):
                    out[x, h, y * rows:(y + 1) * rows] = src[y, h]

    return pl.pallas_call(
        kernel,
        out_shape=jax.ShapeDtypeStruct((X, CHUNKS, Y * rows, LANE), parts.dtype),
        in_specs=[VMEM],
        out_specs=VMEM,
        name="spread_rows",
    )(parts)


def finish(parts, scale):
    hid = parts.shape[2]
    rows = hid // 2

    def kernel(src, out):
        for h in range(CHUNKS):
            for x in range(X):
                at = (h * X + x) * LANE
                out[:, at:at + LANE] = src[x, h].astype(jnp.float32) * scale

    return pl.pallas_call(
        kernel,
        grid=(2,),
        out_shape=jax.ShapeDtypeStruct((hid, CHUNKS * X * LANE), jnp.float32),
        in_specs=[pl.BlockSpec((X, CHUNKS, rows, LANE), lambda i: (0, 0, i, 0))],
        out_specs=pl.BlockSpec((rows, CHUNKS * X * LANE), lambda i: (i, 0)),
        name="finish",
    )(parts)


def per_device(heads, weight, cot):
    xi, yi = lax.axis_index("x"), lax.axis_index("y")
    zl, core, zh = lax.axis_index("zl"), lax.axis_index("core"), lax.axis_index("zh")
    tok, feat = cot.shape
    hid = weight.shape[0]
    blk = tok // ZH
    grad_scale = float(heads.shape[0] * ZH * Y * X) ** (-0.5)

    def order(m, c):
        return (m % ZL) * CORE + c

    rows = [[order(zl, c), order(zl + 2, c), order(zl + 1, c)] for c in (core, 1 - core)]

    sends = [lax.dynamic_slice(cot, ((zh + k) % ZH * blk, 0), (blk, feat)) for k in range(ZH)]
    got = [lax.ppermute(sends[k], ("zl", "core", "zh"), spread_pairs(k)) for k in range(ZH)]

    heads_x = [heads] + [lax.ppermute(heads, "x", ring(X, k)) for k in range(1, X)]
    heads_t = order_heads(heads_x, rows, xi)

    mine = gather_tokens(got, (zh * ROW + zl * CORE + core) % ZH)
    near = []
    for h in range(CHUNKS):
        part = lax.all_to_all(mine[h], "x", 0, 0)
        part = part.reshape(X * blk, ZH * LANE)
        near.append([part] + [lax.ppermute(part, "zl", ring(ZL, k)) for k in (1, 2)])

    wr = hid // Y
    w_part = jnp.concatenate(
        [lax.dynamic_slice(weight, (yi * wr, (h * X + xi) * LANE), (wr, LANE)) for h in range(CHUNKS)], axis=1
    )
    w_far = [lax.ppermute(w_part, "zh", ring(ZH, k)) for k in range(1, ZH)]
    w_y = spread_cols([w_part] + w_far, zh)
    w_y = lax.all_to_all(w_y, "y", 0, 0)
    w_y = weight_rows(w_y)

    owns, oths = [], []
    for h in range(CHUNKS):
        own = jnp.concatenate(near[h], axis=0)
        oth = lax.ppermute(own, "core", ring(CORE, 1))
        owns.append(own)
        oths.append(oth)
    first = weight_part(heads_t, owns[0], oths[0])
    r = weight_part(heads_t, owns[1], oths[1], first)
    r = lax.all_to_all(r.reshape((Y * ZH,) + r.shape[2:]), ("y", "zh"), 0, 0)
    r = spread_sum(r)
    r = lax.all_to_all(r, "y", 0, 0)
    r = spread_rows(r)
    r = lax.all_to_all(r, "x", 0, 0)
    weight_grad = finish(r, grad_scale)

    part = heads_part(owns, oths, w_y, rows, xi)
    part = [part[0]] + [lax.ppermute(part[k], "x", ring(X, k)) for k in range(1, X)]
    head_grad = heads_sum(part)
    return head_grad, weight_grad


def solution(mesh):
    fine = Mesh(mesh.devices.reshape(Y, X, ZL, CORE, ZH), ("y", "x", "zl", "core", "zh"))

    return jax.shard_map(
        per_device,
        mesh=fine,
        in_specs=(P(("y", "x", "zh"), ("zl", "core")), P(("zl", "core"), "zh"), P(("y", "x", "zl", "core"), "zh")),
        out_specs=(P(("y", "x", "zh"), ("zl", "core")), P(("zl", "core"), "zh")),
        check_vma=False,
    )
```
